256 devices in a mesh: dp: 16 (over z_lo, x), expert: 16 (over y, z_hi, core).
Axes of the slice: x: 4, y: 4, z: 8 (z_hi: 2, z_lo: 4; z = z_hi * 4 + z_lo), core: 2. Of those that a mesh axis runs over, the one named last changes fastest.
Arguments:
- tokens: bfloat16 [32768, 2048], P(('dp', 'expert')), may hold values from -24 to 24
- teacher: bfloat16 [32768, 2048], P(('dp', 'expert')), may hold values from -12 to 12
- expert_ids: int32 [32768, 8], P(('dp', 'expert')), may hold values from 0 to 15, all different within a row; in each aligned block of 128 rows (0 to 127, 128 to 255, ...) at most 66 rows name the same one
- route_gates: float32 [32768, 8], P(('dp', 'expert')), may hold values from 0.02 to 0.5
- placement: int32 [16], replicated, may hold values from 0 to 15, as said below
- gate_up_weight: bfloat16 [16, 2048, 768], P('expert'), may hold values from -0.125 to 0.125
- down_weight: bfloat16 [16, 384, 2048], P('expert'), may hold values from -0.3125 to 0.3125
Outputs:
- layer_out: bfloat16 [32768, 2048], P(('dp', 'expert'))
- token_grad: bfloat16 [32768, 2048], P(('dp', 'expert'))
- gate_up_grad: float32 [16, 2048, 768], P('expert', 'dp')
- down_grad: float32 [16, 384, 2048], P('expert', None, 'dp')
The draws below stay inside these ranges and needn't reach their ends.
Inputs may be any that keep to these rules, and one draw needn't show every extreme that they name: `expert_ids`: each row names 8 different experts. Among the rows of one device no expert is named by more than 66 rows, and in every draw some expert is named by exactly 66 rows of some device. `placement`: A permutation of the positions: the devices along expert form pairs, and each pair exchanges one slot of one device with one slot of the other; all other experts e sit at position e.
All inputs are finite; a program needn't handle non-finite values.
Results may differ from the reference program's by a relative error of at most 0.017.
Values may be sent and summed in bfloat16 or wider, within the bound.
No kernel may reach another device: no remote copies, remote signals or barrier semaphores. Data moves between devices by JAX's collectives and lax.ppermute only.
A program may use at most 128 MiB of HBM per device.

```python
import math
import jax
import jax.numpy as jnp
import numpy as np
from jax import lax

D = 2048
FF = 384
TOPK = 8
TOK_DEV = 128
EXP_DEV = 1
EXPERTS = 16
CAP = 66
TOKENS = 32768
N_DP = 16
N_EXPERT = 16


def draw_placement(key, part):
    device_count = EXPERTS // EXP_DEV
    half_count = device_count // 2
    order_key, first_key, second_key = jax.random.split(key, 3)
    device_order = jax.random.permutation(order_key, device_count).astype(jnp.int32)
    first_slot = jax.random.randint(first_key, (half_count,), 0, EXP_DEV, dtype=jnp.int32)
    second_slot = jax.random.randint(second_key, (half_count,), 0, EXP_DEV, dtype=jnp.int32)
    first_position = device_order[0::2] * EXP_DEV + first_slot
    second_position = device_order[1::2] * EXP_DEV + second_slot
    identity = jnp.arange(EXPERTS, dtype=jnp.int32)
    return identity.at[first_position].set(second_position).at[second_position].set(first_position)


def raised(values, rng, source, target, blocks, factor):
    owner, partner = [(jnp.arange(values.shape[axis_at]) // (values.shape[axis_at] // blocks)).reshape([-1 if axis == axis_at else 1 for axis in range(values.ndim)]) for axis_at in (source, target)]
    chosen = jax.random.permutation(rng, blocks)[partner]
    strong = (owner == chosen) | (owner == (partner + blocks // 2) % blocks)
    return jnp.where(strong, factor * values, values)


def block_scale(key, dims, pieces, least, largest):
    level = 1.0
    for axis_at, parts in pieces:
        draws = jax.random.uniform(jax.random.fold_in(jax.random.fold_in(key, 6), axis_at), (parts,), jnp.float32, least / len(pieces), largest / len(pieces))
        level = level * jnp.repeat(jnp.exp(draws), dims[axis_at] // parts).reshape((-1,) + (1,) * (len(dims) - 1 - axis_at))
    return level


def assign_block(key, own, number, rows, number_of, top, most, slope):
    order = jax.random.permutation(key, number_of)
    heavy_load, usual = shares(number_of, rows * top, most, slope, True), shares(number_of, rows * top, most, slope, False)
    places = jnp.arange(number_of)

    def named(lengths, turn):
        used = int((lengths > 0).sum())
        fixed = max(1, used // 4)
        shifted = fixed + (places - fixed + turn * (used - fixed)) % max(1, number_of - fixed)
        return jnp.zeros((number_of,), jnp.int32).at[order[jnp.where(places < fixed, places, shifted)]].set(jnp.asarray(lengths, jnp.int32))

    lengths = jnp.where(number % 4 == 0, named(heavy_load, number // 4), named(usual, number - number // 4 - 1))
    mixed = jax.random.permutation(jax.random.fold_in(own, 3), number_of)
    donor, sink = mixed[0:number_of // 2 * 2:2], mixed[1:number_of // 2 * 2:2]
    margin = jnp.minimum(lengths[donor] - 1, most - lengths[sink]) // 2
    margin = jnp.where((donor == order[0]) | (sink == order[0]) | (lengths[sink] == 0), 0, jnp.maximum(margin, 0))
    shifted = jax.random.randint(jax.random.fold_in(own, 4), (number_of // 2,), 0, 1 << 20) % (margin + 1)
    lengths = lengths.at[donor].add(-shifted).at[sink].add(shifted)
    members = jnp.searchsorted(jnp.cumsum(lengths), jnp.arange(rows * top), side="right").astype(jnp.int32)
    grid = members.reshape(top, rows).T
    grid = grid[jax.random.permutation(jax.random.fold_in(own, 1), rows)]
    turn = jax.random.randint(jax.random.fold_in(own, 2), (rows, 1), 0, top)
    return jnp.take_along_axis(grid, (jnp.arange(top)[None, :] + turn) % top, axis=1)


def shares(count, total, bound, lean, full):
    portions = [(1 << 20) // math.isqrt(grade ** lean) + 1 for grade in range(1, count + 1)]
    largest = bound if full else min(bound, max(-(-total // count), total * portions[0] // sum(portions)))
    least = 1 if total - largest >= count - 1 else 0
    given, surplus = [largest] + [least] * (count - 1), total - largest - least * (count - 1)
    while surplus > 0:
        free = [i for i in range(1, count) if given[i] < largest] or [i for i in range(1, count) if given[i] < bound]
        whole, budget = sum([portions[i] for i in free]), surplus
        for i in free:
            more = min(bound - given[i], max(1, budget * portions[i] // whole), surplus)
            given[i] = given[i] + more
            surplus = surplus - more
    return np.array(given)


def noise(stream_key, shape, spread, bound, cuts=(), kind=jnp.bfloat16):
    drawn = spread * jax.random.normal(stream_key, shape, jnp.float32)
    if cuts:
        drawn = drawn * block_scale(stream_key, shape, cuts, -0.22, 0.18)
    return jnp.clip(drawn, -bound, bound).astype(kind)


def noise_with(rng, shape, width, reach, pieces, heavy, kind=jnp.bfloat16):
    array = width * jax.random.normal(rng, shape, jnp.float32)
    if pieces:
        array = array * block_scale(rng, shape, pieces, -0.22, 0.18)
    return jnp.clip(raised(array, jax.random.fold_in(rng, 3), *heavy), -reach, reach).astype(kind)


def setup_inputs(seed: int = 0) -> dict:
    streams_of = jax.random.split(jax.random.key(seed), 8)
    tokens = noise_with(streams_of[0], (TOKENS, D), 1.0, 24.0, ((0, 256),), (0, 1, 256, 6.0))
    teacher = noise_with(streams_of[1], (TOKENS, D), 0.5, 12.0, ((0, 256),), (0, 1, 256, 6.0))
    expert_ids_keys = jax.random.split(jax.random.fold_in(streams_of[2], 1), TOKENS // TOK_DEV)
    expert_ids_turns = jax.random.permutation(jax.random.fold_in(streams_of[2], 3), TOKENS // TOK_DEV)
    expert_ids = jax.vmap(lambda own, number: assign_block(jax.random.fold_in(streams_of[2], 2), own, number, TOK_DEV, EXPERTS, TOPK, CAP, 2))(expert_ids_keys, expert_ids_turns).reshape((TOKENS, TOPK))
    route_gates = jnp.clip(jnp.exp(math.log(0.5) - 3.218876 * jax.random.uniform(streams_of[3], (TOKENS, TOPK), jnp.float32) ** block_scale(streams_of[3], (TOKENS, TOPK), ((0, 256),), -0.2, 0.2)), 0.02, 0.5)
    placement = draw_placement(jax.random.fold_in(streams_of[7], 71), 0)
    gate_up_weight = noise(streams_of[5], (EXPERTS, D, 2 * FF), D ** -0.5, 0.125, ((0, 16),))
    down_weight = noise(streams_of[6], (EXPERTS, FF, D), FF ** -0.5, 0.3125, ((0, 16),))
    return {"tokens": tokens, "teacher": teacher, "expert_ids": expert_ids, "route_gates": route_gates, "placement": placement, "gate_up_weight": gate_up_weight, "down_weight": down_weight}


def silu_parts(gate_pre):
    sigmoid_val = jax.nn.sigmoid(gate_pre)
    return gate_pre * sigmoid_val, sigmoid_val * (1.0 + gate_pre * (1.0 - sigmoid_val))


def round_keep(value):
    return lax.optimization_barrier(value.astype(jnp.bfloat16)).astype(jnp.float32)


def reference(tokens, teacher, expert_ids, route_gates, placement, gate_up_weight, down_weight):
    group_rows = TOK_DEV * N_EXPERT
    group_slots = N_EXPERT * CAP
    pad_index = group_rows * TOPK
    token_groups = jnp.concatenate([tokens.reshape(N_DP, group_rows, D), jnp.zeros((N_DP, 1, D), jnp.bfloat16)], axis=1)
    id_groups = expert_ids.reshape(N_DP, group_rows * TOPK)
    gate_groups = jnp.concatenate([route_gates.reshape(N_DP, group_rows * TOPK), jnp.zeros((N_DP, 1), jnp.float32)], axis=1)
    group_index = jnp.arange(N_DP, dtype=jnp.int32)[:, None]
    all_experts = jnp.arange(EXPERTS, dtype=jnp.int32)
    positions = jnp.arange(EXPERTS, dtype=jnp.int32)

    def expert_forward(position):
        expert = jnp.sum(jnp.where(placement == position, all_experts, 0)).astype(jnp.int32)

        def one_group(ids_row):
            return jnp.nonzero(ids_row == expert, size=group_slots, fill_value=pad_index)[0].astype(jnp.int32)

        flat_index = jax.vmap(one_group)(id_groups)
        token_index = (flat_index // TOPK).astype(jnp.int32)
        inputs = token_groups[group_index, token_index]
        pre_act = jnp.einsum('grd,df->grf', inputs.astype(jnp.float32), gate_up_weight[position].astype(jnp.float32))
        activation, silu_slope = silu_parts(pre_act[..., :FF])
        up_part = pre_act[..., FF:]
        hidden = (activation * up_part).astype(jnp.bfloat16)
        return flat_index, token_index, inputs, activation, silu_slope, up_part, hidden

    def forward_step(running, position):
        flat_index, token_index, inputs, activation, silu_slope, up_part, hidden = expert_forward(position)
        expert_out = jnp.einsum('grf,fd->grd', hidden.astype(jnp.float32), down_weight[position].astype(jnp.float32)).astype(jnp.bfloat16)
        weight = gate_groups[group_index, flat_index]
        running = running.at[group_index, token_index].add(weight[..., None] * expert_out.astype(jnp.float32))
        return running, None

    zero_start = jnp.zeros((N_DP, group_rows + 1, D), jnp.float32)
    summed, _ = lax.scan(forward_step, zero_start, positions)
    layer_sum = summed[:, :group_rows].reshape(TOKENS, D)
    layer_out = layer_sum.astype(jnp.bfloat16)
    residual = layer_sum - teacher.astype(jnp.float32)
    residual_groups = jnp.concatenate([residual.reshape(N_DP, group_rows, D), jnp.zeros((N_DP, 1, D), jnp.float32)], axis=1)

    def backward_step(running, position):
        flat_index, token_index, inputs, activation, silu_slope, up_part, hidden = expert_forward(position)
        weight = gate_groups[group_index, flat_index]
        grad_rows = (weight[..., None] * residual_groups[group_index, token_index]).astype(jnp.bfloat16)
        grad_hidden = jnp.einsum('grd,fd->grf', grad_rows.astype(jnp.float32), down_weight[position].astype(jnp.float32))
        grad_mixed = jnp.concatenate([grad_hidden * up_part * silu_slope, grad_hidden * activation], axis=-1).astype(jnp.bfloat16)
        row_grads = jnp.einsum('grf,df->grd', grad_mixed.astype(jnp.float32), gate_up_weight[position].astype(jnp.float32)).astype(jnp.bfloat16)
        running = running.at[group_index, token_index].add(row_grads.astype(jnp.float32))
        down_part = jnp.einsum('grf,grd->gfd', hidden.astype(jnp.float32), grad_rows.astype(jnp.float32))
        input_part = jnp.einsum('grd,grf->gdf', inputs.astype(jnp.float32), grad_mixed.astype(jnp.float32))
        return running, (jnp.sum(round_keep(input_part), axis=0), jnp.sum(round_keep(down_part), axis=0))

    grad_sum, (gate_up_grad, down_grad) = lax.scan(backward_step, zero_start, positions)
    token_grad = grad_sum[:, :group_rows].reshape(TOKENS, D).astype(jnp.bfloat16)
    return (layer_out, token_grad, gate_up_grad, down_grad)
```

```python
import jax
import jax.numpy as jnp
from jax import lax
from jax.sharding import PartitionSpec as P


BF = jnp.bfloat16
F32 = jnp.float32
NY = 4
NX = 4
NZ = 4


def expert_perm(dy, dz, dc):
    out = []
    for y in range(NY):
        for z in range(2):
            for c in range(2):
                src = ((y + dy) % NY) * 4 + (z ^ dz) * 2 + (c ^ dc)
                out.append((src, y * 4 + z * 2 + c))
    return out


def dp_perm(dzl, dx):
    out = []
    for z in range(NZ):
        for x in range(NX):
            src = ((z + dzl) % NZ) * NX + (x + dx) % NX
            out.append((src, z * NX + x))
    return out


def from_expert(value, dy, dz, dc):
    return lax.ppermute(value, "expert", expert_perm(dy, dz, dc))


def from_dp(value, dzl, dx):
    return lax.ppermute(value, "dp", dp_perm(dzl, dx))


def mm(a, b, dims):
    return lax.dot_general(a, b, (dims, ((), ())), preferred_element_type=F32)


def gather_rows(own):
    far = from_expert(own, 0, 1, 0)
    out = []
    for start in (own, far):
        half = jnp.concatenate([start] + [from_expert(start, dy, 0, 0) for dy in (1, 2, 3)], axis=0)
        out.append((half, from_expert(half, 0, 0, 1)))
    return out


def scatter_rows(parts, rows):
    sums = [None, None]
    for dz in (1, 0):
        other = from_expert(parts(dz, 1).astype(BF), 0, 0, 1)
        both = (parts(dz, 0) + other.astype(F32)).astype(BF)
        total = both[:rows].astype(F32)
        for dy in (1, 2, 3):
            block = lax.slice_in_dim(both, dy * rows, (dy + 1) * rows, axis=0)
            total = total + from_expert(block, -dy, 0, 0).astype(F32)
        sums[dz] = total
    return sums[0] + from_expert(sums[1].astype(BF), 0, 1, 0).astype(F32)


def scatter_grad(term):
    index = lax.axis_index("dp")
    x_at, z_at = index % NX, index // NX
    width = term.shape[1]
    blocks = term.astype(BF).reshape(NZ, NX, -1, width)
    total = lax.dynamic_index_in_dim(blocks, x_at, 1, keepdims=False).astype(F32)
    for dx in (2, 1, 3):
        part = lax.dynamic_index_in_dim(blocks, (x_at + dx) % NX, 1, keepdims=False)
        total = total + from_dp(part, 0, -dx).astype(F32)
    result = lax.dynamic_index_in_dim(total, z_at, 0, keepdims=False)
    rounded = total.astype(BF)
    for dzl in (2, 1, 3):
        part = lax.dynamic_index_in_dim(rounded, (z_at + dzl) % NZ, 0, keepdims=False)
        result = result + from_dp(part, -dzl, 0).astype(F32)
    return result


def shards(tokens, teacher, expert_ids, route_gates, placement, gate_up_weight, down_weight):
    rows = tokens.shape[0]
    w_gu = gate_up_weight[0]
    w_dn = down_weight[0]
    ff = w_dn.shape[0]
    count = lax.axis_size("expert")
    token_rows = gather_rows(tokens)

    table = jnp.arange(count, dtype=jnp.int32)
    chosen = expert_ids[:, :, None] == table
    position = jnp.sum(jnp.where(chosen, placement, 0), axis=2)
    gate_of = jnp.sum(
        jnp.where(table[:, None, None] == position[None], route_gates[None], 0.0), axis=2
    )
    gate_in = lax.all_to_all(gate_of, "expert", split_axis=0, concat_axis=0, tiled=True)
    here = lax.axis_index("expert")
    y_at, z_at, c_at = here // 4, (here // 2) % 2, here % 2

    def gates(dz, dc):
        out = []
        for dy in range(NY):
            src = ((y_at + dy) % NY) * 4 + (z_at ^ dz) * 2 + (c_at ^ dc)
            out.append(jnp.sum(jnp.where(table[:, None] == src, gate_in, 0.0), axis=0))
        return jnp.concatenate(out)[:, None]

    saved = {}

    def forward(dz, dc):
        pre = mm(token_rows[dz][dc], w_gu, ((1,), (0,)))
        g, u = pre[:, :ff], pre[:, ff:]
        s = jax.nn.sigmoid(g)
        gate = gates(dz, dc)
        hidden = (gate * (g * s) * u).astype(BF)
        saved[dz, dc] = (pre, gate, hidden)
        return mm(hidden, w_dn, ((1,), (0,)))

    layer_sum = scatter_rows(forward, rows)
    layer_out = layer_sum.astype(BF)
    residual = (layer_sum - teacher.astype(F32)).astype(BF)
    res_rows = gather_rows(residual)

    mixed = {}
    input_term = None
    down_term = None
    for dz in (0, 1):
        for dc in (0, 1):
            pre, gate, hidden = saved[dz, dc]
            g, u = pre[:, :ff], pre[:, ff:]
            s = jax.nn.sigmoid(g)
            grad = gate * mm(res_rows[dz][dc], w_dn, ((1,), (1,)))
            mixed[dz, dc] = jnp.concatenate(
                [grad * u * (s * (1.0 + g * (1.0 - s))), grad * (g * s)], axis=1
            ).astype(BF)
            down_part = mm(res_rows[dz][dc], hidden, ((0,), (0,)))
            input_part = mm(token_rows[dz][dc], mixed[dz, dc], ((0,), (0,)))
            down_term = down_part if down_term is None else down_term + down_part
            input_term = input_part if input_term is None else input_term + input_part

    down_share = scatter_grad(down_term)
    input_share = scatter_grad(input_term)
    token_sum = scatter_rows(lambda dz, dc: mm(mixed[dz, dc], w_gu, ((1,), (1,))), rows)
    return (layer_out, token_sum.astype(BF), input_share[None], down_share.T[None])


def solution(mesh):
    in_specs = (
        P(("dp", "expert"), None),
        P(("dp", "expert"), None),
        P(("dp", "expert"), None),
        P(("dp", "expert"), None),
        P(),
        P("expert", None, None),
        P("expert", None, None),
    )
    out_specs = (
        P(("dp", "expert"), None),
        P(("dp", "expert"), None),
        P("expert", "dp", None),
        P("expert", None, "dp"),
    )
    return jax.shard_map(shards, mesh=mesh, in_specs=in_specs, out_specs=out_specs, check_vma=False)
```

```python
import jax
import jax.numpy as jnp
from jax import lax
from jax.sharding import PartitionSpec as P


BF = jnp.bfloat16
F32 = jnp.float32
NY = 4
NX = 4
NZ = 4


def expert_perm(dy, dz, dc):
    out = []
    for y in range(NY):
        for z in range(2):
            for c in range(2):
                src = ((y + dy) % NY) * 4 + (z ^ dz) * 2 + (c ^ dc)
                out.append((src, y * 4 + z * 2 + c))
    return out


def dp_perm(dzl, dx):
    out = []
    for z in range(NZ):
        for x in range(NX):
            src = ((z + dzl) % NZ) * NX + (x + dx) % NX
            out.append((src, z * NX + x))
    return out


def from_expert(value, dy, dz, dc):
    return lax.ppermute(value, "expert", expert_perm(dy, dz, dc))


def from_dp(value, dzl, dx):
    return lax.ppermute(value, "dp", dp_perm(dzl, dx))


def mm(a, b, dims):
    return lax.dot_general(a, b, (dims, ((), ())), preferred_element_type=F32)


def tie(*values):
    return lax.optimization_barrier(values)


def gather_y(start):
    blocks = [start] + [from_expert(start, dy, 0, 0) for dy in (2, 1, 3)]
    return jnp.concatenate([blocks[0], blocks[2], blocks[1], blocks[3]], axis=0)


def scatter_y(both, own, rows):
    total = own[:rows].astype(F32)
    for dy in (2, 1, 3):
        block = lax.slice_in_dim(both, dy * rows, (dy + 1) * rows, axis=0)
        total = total + from_expert(block, -dy, 0, 0).astype(F32)
    return total


def across(value):
    return from_expert(value, 0, 0, 1)


def joined(part, other):
    return (part + across(other.astype(BF)).astype(F32)).astype(BF)


def x_stage(term):
    x_at = lax.axis_index("dp") % NX
    blocks = term.astype(BF).reshape(NZ, NX, -1, term.shape[1])
    own = lax.dynamic_index_in_dim(blocks, x_at, 1, keepdims=False)
    got = []
    for dx in (2, 1, 3):
        part = lax.dynamic_index_in_dim(blocks, (x_at + dx) % NX, 1, keepdims=False)
        got.append(from_dp(part, 0, -dx))
    return own, got


def z_stage(total):
    z_at = lax.axis_index("dp") // NX
    result = lax.dynamic_index_in_dim(total, z_at, 0, keepdims=False)
    rounded = total.astype(BF)
    for dzl in (2, 1, 3):
        part = lax.dynamic_index_in_dim(rounded, (z_at + dzl) % NZ, 0, keepdims=False)
        result = result + from_dp(part, -dzl, 0).astype(F32)
    return result


def shards(tokens, teacher, expert_ids, route_gates, placement, gate_up_weight, down_weight):
    rows = tokens.shape[0]
    w_gu = gate_up_weight[0]
    w_dn = down_weight[0]
    ff = w_dn.shape[0]
    count = lax.axis_size("expert")
    here = lax.axis_index("expert")
    y_at, z_at, c_at = here // 4, (here // 2) % 2, here % 2

    table = jnp.arange(count, dtype=jnp.int32)
    chosen = expert_ids[:, :, None] == table
    position = jnp.sum(jnp.where(chosen, placement, 0), axis=2)
    gate_of = jnp.sum(
        jnp.where(table[:, None, None] == position[None], route_gates[None], 0.0), axis=2
    )

    far_rows = from_expert(tokens, 0, 1, 0)
    near = gather_y(tokens)
    gate_in = lax.all_to_all(gate_of, "expert", split_axis=0, concat_axis=0, tiled=True)
    near, far_rows, gate_in = tie(near, far_rows, gate_in)

    def gates(dz, dc):
        out = []
        for dy in range(NY):
            src = ((y_at + dy) % NY) * 4 + (z_at ^ dz) * 2 + (c_at ^ dc)
            out.append(jnp.sum(jnp.where(table[:, None] == src, gate_in, 0.0), axis=0))
        return jnp.concatenate(out)[:, None]

    def forward(row_block, gate):
        pre = mm(row_block, w_gu, ((1,), (0,)))
        g, u = pre[:, :ff], pre[:, ff:]
        s = jax.nn.sigmoid(g)
        hidden = (gate * (g * s) * u).astype(BF)
        return pre, hidden, mm(hidden, w_dn, ((1,), (0,)))

    def backward(res_block, saved):
        pre, gate = saved
        g, u = pre[:, :ff], pre[:, ff:]
        s = jax.nn.sigmoid(g)
        grad = gate * mm(res_block, w_dn, ((1,), (1,)))
        return jnp.concatenate(
            [grad * u * (s * (1.0 + g * (1.0 - s))), grad * (g * s)], axis=1
        ).astype(BF)

    def gate_up_part(row_blocks, mixed):
        return mm(row_blocks[0], mixed[0], ((0,), (0,))) + mm(row_blocks[1], mixed[1], ((0,), (0,)))

    gate = [[gates(dz, dc) for dc in (0, 1)] for dz in (0, 1)]
    saved = [[None, None], [None, None]]
    hidden = [[None, None], [None, None]]

    far = gather_y(far_rows)
    row_blocks = [[near, across(near)], None]
    both = [None, None]
    for dz in (0, 1):
        if dz == 1:
            far, near_own = tie(far, both[0])
            row_blocks[1] = [far, across(far)]
        outs = [None, None]
        for dc in (1, 0):
            pre, hidden[dz][dc], outs[dc] = forward(row_blocks[dz][dc], gate[dz][dc])
            saved[dz][dc] = (pre, gate[dz][dc])
        both[dz] = joined(outs[0], outs[1])
    far_sum = scatter_y(both[1], both[1], rows)
    near_sum = scatter_y(both[0], near_own, rows)
    layer_sum = near_sum + from_expert(far_sum.astype(BF), 0, 1, 0).astype(F32)
    layer_out = layer_sum.astype(BF)
    residual = (layer_sum - teacher.astype(F32)).astype(BF)

    far_res = from_expert(residual, 0, 1, 0)
    near_res = gather_y(residual)
    near_res, far_res = tie(near_res, far_res)
    far_res = gather_y(far_res)
    res = [near_res, across(near_res)]
    mixed = [backward(res[dc], saved[0][dc]) for dc in (0, 1)]
    grads = [mm(mixed[dc], w_gu, ((1,), (1,))) for dc in (0, 1)]
    near_both = joined(grads[0], grads[1])
    down_term = mm(res[0], hidden[0][0], ((0,), (0,))) + mm(res[1], hidden[0][1], ((0,), (0,)))
    input_term = gate_up_part(row_blocks[0], mixed)
    far_res, near_own, down_term, input_term = tie(far_res, near_both, down_term, input_term)
    near_sum = scatter_y(near_both, near_own, rows)

    res = [far_res, across(far_res)]
    mixed = [backward(res[dc], saved[1][dc]) for dc in (0, 1)]
    down_term = down_term + (
        mm(res[0], hidden[1][0], ((0,), (0,))) + mm(res[1], hidden[1][1], ((0,), (0,)))
    )
    input_term = input_term + gate_up_part(row_blocks[1], mixed)
    down_own, down_got = x_stage(down_term)
    input_own, input_got = x_stage(input_term)
    grads = [mm(mixed[dc], w_gu, ((1,), (1,))) for dc in (0, 1)]
    far_both = joined(grads[0], grads[1])
    far_own, down_got, input_got = tie(far_both, down_got, input_got)
    far_sum = scatter_y(far_both, far_own, rows)

    def added(own, got):
        total = own.astype(F32)
        for part in got:
            total = total + part.astype(F32)
        return total

    share = z_stage(
        jnp.concatenate([added(input_own, input_got), added(down_own, down_got)], axis=2)
    )
    token_sum = near_sum + from_expert(far_sum.astype(BF), 0, 1, 0).astype(F32)
    split = 2 * ff
    return (layer_out, token_sum.astype(BF), share[None, :, :split], share[:, split:].T[None])


def solution(mesh):
    in_specs = (
        P(("dp", "expert"), None),
        P(("dp", "expert"), None),
        P(("dp", "expert"), None),
        P(("dp", "expert"), None),
        P(),
        P("expert", None, None),
        P("expert", None, None),
    )
    out_specs = (
        P(("dp", "expert"), None),
        P(("dp", "expert"), None),
        P("expert", "dp", None),
        P("expert", None, "dp"),
    )
    return jax.shard_map(shards, mesh=mesh, in_specs=in_specs, out_specs=out_specs, check_vma=False)
```

```python
import jax
import jax.numpy as jnp
from jax import lax
from jax.experimental import pallas as pl
from jax.sharding import PartitionSpec as P


BF = jnp.bfloat16
F32 = jnp.float32
NY = 4
NX = 4
NZ = 4


def expert_perm(dy, dz, dc):
    out = []
    for y in range(NY):
        for z in range(2):
            for c in range(2):
                src = ((y + dy) % NY) * 4 + (z ^ dz) * 2 + (c ^ dc)
                out.append((src, y * 4 + z * 2 + c))
    return out


def dp_perm(dzl, dx):
    out = []
    for z in range(NZ):
        for x in range(NX):
            src = ((z + dzl) % NZ) * NX + (x + dx) % NX
            out.append((src, z * NX + x))
    return out


def from_expert(value, dy, dz, dc):
    return lax.ppermute(value, "expert", expert_perm(dy, dz, dc))


def from_dp(value, dzl, dx):
    return lax.ppermute(value, "dp", dp_perm(dzl, dx))


def mm(a, b, dims):
    return lax.dot_general(a, b, (dims, ((), ())), preferred_element_type=F32)


def tie(*values):
    return lax.optimization_barrier(values)


def gather_y(start):
    blocks = [start] + [from_expert(start, dy, 0, 0) for dy in (2, 1, 3)]
    return jnp.concatenate([blocks[0], blocks[2], blocks[1], blocks[3]], axis=0)


def scatter_y(blocks, own):
    total = own.astype(F32)
    for dy in (2, 1, 3):
        total = total + from_expert(blocks[dy], -dy, 0, 0).astype(F32)
    return total


def across(value):
    return from_expert(value, 0, 0, 1)


def joined(part, other, rows):
    got = across(other.astype(BF))
    out = []
    for dy in range(NY):
        at = slice(dy * rows, (dy + 1) * rows)
        out.append((part[at].astype(F32) + got[at].astype(F32)).astype(BF))
    return out


def grad_kernel(t0, t1, r0, r1, m0, m1, h0, h1, *rest):
    acc, out = rest if len(rest) == 2 else (None, rest[0])
    wide = m0.shape[1]
    dims = ((0,), (0,))
    left = mm(t0[...], m0[...], dims) + mm(t1[...], m1[...], dims)
    right = mm(r0[...], h0[...], dims) + mm(r1[...], h1[...], dims)
    if acc is not None:
        left = left + acc[:, :wide]
        right = right + acc[:, wide:]
    out[:, :wide] = left.astype(out.dtype)
    out[:, wide:] = right.astype(out.dtype)


def back_kernel(res, pre, gate, w_gu, w_dn, mixed, out):
    ff = w_dn.shape[0]
    grad = gate[...] * mm(res[...], w_dn[...], ((1,), (1,)))
    g, u = pre[:, :ff], pre[:, ff:]
    s = jax.nn.sigmoid(g)
    mixed[:, :ff] = (grad * u * (s * (1.0 + g * (1.0 - s)))).astype(BF)
    mixed[:, ff:] = (grad * (g * s)).astype(BF)
    out[...] = mm(mixed[...], w_gu[...], ((1,), (1,))).astype(BF)


def backward(res, saved, w_gu, w_dn):
    pre, gate = saved
    count, features = res.shape
    wide = pre.shape[1]
    tile = min(256, count)

    def rows_of(width):
        return pl.BlockSpec((tile, width), lambda i: (i, 0))

    def whole(array):
        return pl.BlockSpec(array.shape, lambda i: (0, 0))

    return pl.pallas_call(
        back_kernel,
        grid=(count // tile,),
        in_specs=[rows_of(features), rows_of(wide), rows_of(1), whole(w_gu), whole(w_dn)],
        out_specs=[rows_of(wide), rows_of(features)],
        out_shape=[
            jax.ShapeDtypeStruct((count, wide), BF),
            jax.ShapeDtypeStruct((count, features), BF),
        ],
        name="backward_rows",
        cost_estimate=pl.CostEstimate(
            flops=3 * count * features * wide,
            transcendentals=count * wide // 2,
            bytes_accessed=4 * count * features + 6 * count * wide + 3 * features * wide,
        ),
    )(res, pre, gate, w_gu, w_dn)


def weight_grads(row_blocks, res, mixed, hidden, acc):
    count, features = row_blocks[0].shape
    wide, narrow = mixed[0].shape[1], hidden[0].shape[1]
    tile = min(256, features)
    column = pl.BlockSpec((count, tile), lambda i: (0, i))
    out_spec = pl.BlockSpec((tile, wide + narrow), lambda i: (i, 0))
    args = [*row_blocks, *res, *mixed, *hidden]
    specs = [column] * 4 + [pl.BlockSpec((count, wide), lambda i: (0, 0))] * 2
    specs += [pl.BlockSpec((count, narrow), lambda i: (0, 0))] * 2
    if acc is not None:
        args.append(acc)
        specs.append(out_spec)
    kind = F32 if acc is None else BF
    return pl.pallas_call(
        grad_kernel,
        grid=(features // tile,),
        in_specs=specs,
        out_specs=out_spec,
        out_shape=jax.ShapeDtypeStruct((features, wide + narrow), kind),
        name="weight_grads",
        cost_estimate=pl.CostEstimate(
            flops=4 * count * features * (wide + narrow),
            transcendentals=0,
            bytes_accessed=8 * count * features + 8 * features * (wide + narrow),
        ),
    )(*args)


def x_stage(term):
    x_at = lax.axis_index("dp") % NX
    blocks = term.reshape(NZ, NX, -1, term.shape[1])
    own = lax.dynamic_index_in_dim(blocks, x_at, 1, keepdims=False)
    got = []
    for dx in (2, 1, 3):
        part = lax.dynamic_index_in_dim(blocks, (x_at + dx) % NX, 1, keepdims=False)
        got.append(from_dp(part, 0, -dx))
    return own, got


def z_stage(total):
    z_at = lax.axis_index("dp") // NX
    result = lax.dynamic_index_in_dim(total, z_at, 0, keepdims=False)
    rounded = total.astype(BF)
    for dzl in (2, 1, 3):
        part = lax.dynamic_index_in_dim(rounded, (z_at + dzl) % NZ, 0, keepdims=False)
        result = result + from_dp(part, -dzl, 0).astype(F32)
    return result


def shards(tokens, teacher, expert_ids, route_gates, placement, gate_up_weight, down_weight):
    rows = tokens.shape[0]
    w_gu = gate_up_weight[0]
    w_dn = down_weight[0]
    ff = w_dn.shape[0]
    count = lax.axis_size("expert")
    here = lax.axis_index("expert")
    y_at, z_at, c_at = here // 4, (here // 2) % 2, here % 2

    table = jnp.arange(count, dtype=jnp.int32)
    chosen = expert_ids[:, :, None] == table
    position = jnp.sum(jnp.where(chosen, placement, 0), axis=2)
    gate_of = jnp.sum(
        jnp.where(table[:, None, None] == position[None], route_gates[None], 0.0), axis=2
    )

    far_rows = from_expert(tokens, 0, 1, 0)
    near = gather_y(tokens)
    gate_in = lax.all_to_all(gate_of, "expert", split_axis=0, concat_axis=0, tiled=True)
    near, far_rows, gate_in = tie(near, far_rows, gate_in)

    def gates(dz, dc):
        out = []
        for dy in range(NY):
            src = ((y_at + dy) % NY) * 4 + (z_at ^ dz) * 2 + (c_at ^ dc)
            out.append(jnp.sum(jnp.where(table[:, None] == src, gate_in, 0.0), axis=0))
        return jnp.concatenate(out)[:, None]

    def forward(row_block, gate):
        pre = mm(row_block, w_gu, ((1,), (0,)))
        g, u = pre[:, :ff], pre[:, ff:]
        s = jax.nn.sigmoid(g)
        hidden = (gate * (g * s) * u).astype(BF)
        return pre, hidden, mm(hidden, w_dn, ((1,), (0,)))

    gate = [[gates(dz, dc) for dc in (0, 1)] for dz in (0, 1)]
    saved = [[None, None], [None, None]]
    hidden = [[None, None], [None, None]]

    far = gather_y(far_rows)
    row_blocks = [[near, across(near)], None]
    both = [None, None]
    for dz in (0, 1):
        if dz == 1:
            far, near_own = tie(far, both[0][0])
            row_blocks[1] = [far, across(far)]
        outs = [None, None]
        for dc in (1, 0):
            pre, hidden[dz][dc], outs[dc] = forward(row_blocks[dz][dc], gate[dz][dc])
            saved[dz][dc] = (pre, gate[dz][dc])
        both[dz] = joined(outs[0], outs[1], rows)
    far_sum = scatter_y(both[1], both[1][0])
    near_sum = scatter_y(both[0], near_own)
    layer_sum = near_sum + from_expert(far_sum.astype(BF), 0, 1, 0).astype(F32)
    layer_out = layer_sum.astype(BF)
    residual = (layer_sum - teacher.astype(F32)).astype(BF)

    far_res = from_expert(residual, 0, 1, 0)
    near_res = gather_y(residual)
    near_res, far_res = tie(near_res, far_res)
    far_res = gather_y(far_res)
    res = [near_res, across(near_res)]
    near_pairs = [backward(res[dc], saved[0][dc], w_gu, w_dn) for dc in (0, 1)]
    mixed = [pair[0] for pair in near_pairs]
    near_both = joined(near_pairs[0][1], near_pairs[1][1], rows)
    near_sum = scatter_y(near_both, near_both[0])
    term = weight_grads(row_blocks[0], res, mixed, hidden[0], None)

    res = [far_res, across(far_res)]
    pairs = [backward(res[dc], saved[1][dc], w_gu, w_dn) for dc in (0, 1)]
    mixed = [pair[0] for pair in pairs]
    term = weight_grads(row_blocks[1], res, mixed, hidden[1], term)
    own, got = x_stage(term)
    far_both = joined(pairs[0][1], pairs[1][1], rows)
    far_sum = scatter_y(far_both, far_both[0]).astype(BF)
    crossed = from_expert(far_sum, 0, 1, 0)

    total = own.astype(F32)
    for part in got:
        total = total + part.astype(F32)
    share = z_stage(total)
    token_sum = near_sum + crossed.astype(F32)
    split = 2 * ff
    return (layer_out, token_sum.astype(BF), share[None, :, :split], share[:, split:].T[None])


def solution(mesh):
    in_specs = (
        P(("dp", "expert"), None),
        P(("dp", "expert"), None),
        P(("dp", "expert"), None),
        P(("dp", "expert"), None),
        P(),
        P("expert", None, None),
        P("expert", None, None),
    )
    out_specs = (
        P(("dp", "expert"), None),
        P(("dp", "expert"), None),
        P("expert", "dp", None),
        P("expert", None, "dp"),
    )

    return jax.shard_map(shards, mesh=mesh, in_specs=in_specs, out_specs=out_specs, check_vma=False)
```

```python
import functools

import jax
import jax.numpy as jnp
from jax import lax
from jax.experimental import pallas as pl
from jax.experimental.pallas import tpu as pltpu
from jax.sharding import PartitionSpec as P


BF = jnp.bfloat16
F32 = jnp.float32
NY = 4
NX = 4
NZ = 4


def expert_perm(dy, dz, dc):
    out = []
    for y in range(NY):
        for z in range(2):
            for c in range(2):
                src = ((y + dy) % NY) * 4 + (z ^ dz) * 2 + (c ^ dc)
                out.append((src, y * 4 + z * 2 + c))
    return out


def dp_perm(dzl, dx):
    out = []
    for z in range(NZ):
        for x in range(NX):
            src = ((z + dzl) % NZ) * NX + (x + dx) % NX
            out.append((src, z * NX + x))
    return out


def from_expert(value, dy, dz, dc):
    return lax.ppermute(value, "expert", expert_perm(dy, dz, dc))


def from_dp(value, dzl, dx):
    return lax.ppermute(value, "dp", dp_perm(dzl, dx))


def mm(a, b, dims):
    return lax.dot_general(a, b, (dims, ((), ())), preferred_element_type=F32)


def tie(*values):
    return lax.optimization_barrier(values)


def gather_y(start):
    blocks = [start] + [from_expert(start, dy, 0, 0) for dy in (2, 1, 3)]
    return jnp.concatenate([blocks[0], blocks[2], blocks[1], blocks[3]], axis=0)


def scatter_y(blocks, own):
    total = own.astype(F32)
    for dy in (2, 1, 3):
        total = total + from_expert(blocks[dy], -dy, 0, 0).astype(F32)
    return total


def across(value):
    return from_expert(value, 0, 0, 1)


def joined(part, other, rows):
    got = across(other.astype(BF))
    out = []
    for dy in range(NY):
        at = slice(dy * rows, (dy + 1) * rows)
        out.append((part[at].astype(F32) + got[at].astype(F32)).astype(BF))
    return out


LANES = 128


def grad_kernel(x_ref, *refs, first):
    columns, refs = refs[:8], refs[8:]
    sides, refs = refs[:6], refs[6:]
    acc, refs = (None, refs) if first else (refs[0], refs[1:])
    outs, turned = refs[:-1], refs[-1]
    ff = sides[0].shape[1]

    @pl.when((pl.program_id(0) == 0) & (pl.program_id(1) == 0))
    def _():
        for k in range(6):
            turned[k] = sides[k][...].astype(F32).T.astype(BF)

    def product(k, at):
        wide = jnp.concatenate([columns[at][...], columns[at + 1][...]], axis=1)
        return mm(turned[k], wide, ((1,), (0,)))

    parts = [
        product(0, 0) + product(3, 2),
        product(1, 0) + product(4, 2),
        product(2, 4) + product(5, 6),
    ]

    def store(out, *lead):
        for k in range(3):
            rows = slice(k * ff, (k + 1) * ff)
            for z in range(2):
                value = parts[k][:, z * LANES : (z + 1) * LANES]
                if acc is not None:
                    value = value + acc[0, z, rows, :]
                out[(*lead, z, rows, slice(None))] = value.astype(out.dtype)

    if first:
        store(outs[0], 0)
    else:
        for k in range(NX):

            @pl.when(pl.program_id(0) == k)
            def _(k=k):
                store(outs[k])


def weight_grads(row_blocks, res, sides, acc):
    count, features = row_blocks[0].shape
    ff = sides[0].shape[1]
    x_at = (lax.axis_index("dp") % NX).astype(jnp.int32).reshape(1)

    def column(second):
        return pl.BlockSpec(
            (count, LANES),
            lambda i, j, x: (0, (2 * j + second) * NX + (x[0] + i) % NX),
        )

    args, specs = [], []
    for array in (*row_blocks, *res):
        args += [array, array]
        specs += [column(0), column(1)]
    args += sides
    specs += [pl.BlockSpec((count, ff), lambda i, j, x: (0, 0))] * 6
    whole = (NX, NZ, 3 * ff, LANES)
    acc_spec = pl.BlockSpec((1, 2, 3 * ff, LANES), lambda i, j, x: (i, j, 0, 0))
    if acc is None:
        out_specs = [acc_spec]
        out_shape = [jax.ShapeDtypeStruct(whole, F32)]
    else:
        args.append(acc)
        specs.append(acc_spec)

        def block_of(k):
            def index(i, j, x):
                return (jnp.where(i == k, j, jnp.where(i < k, 0, 1)), 0, 0)

            return pl.BlockSpec((2, 3 * ff, LANES), index)

        out_specs = [block_of(k) for k in range(NX)]
        out_shape = [jax.ShapeDtypeStruct(whole[1:], BF)] * NX
    return pl.pallas_call(
        functools.partial(grad_kernel, first=acc is None),
        grid_spec=pltpu.PrefetchScalarGridSpec(
            num_scalar_prefetch=1,
            grid=(NX, NZ // 2),
            in_specs=specs,
            out_specs=out_specs,
            scratch_shapes=[pltpu.VMEM((6, ff, count), BF)],
        ),
        out_shape=out_shape,
        name="weight_grads",
        cost_estimate=pl.CostEstimate(
            flops=12 * count * features * ff,
            transcendentals=0,
            bytes_accessed=8 * count * features + 24 * features * ff,
        ),
    )(x_at, *args)


def x_stage(blocks):
    return [from_dp(blocks[dx], 0, -dx) for dx in (2, 1, 3)]


def z_stage(total):
    z_at = lax.axis_index("dp") // NX
    result = lax.dynamic_index_in_dim(total, z_at, 0, keepdims=False)
    rounded = total.astype(BF)
    for dzl in (2, 1, 3):
        part = lax.dynamic_index_in_dim(rounded, (z_at + dzl) % NZ, 0, keepdims=False)
        result = result + from_dp(part, -dzl, 0).astype(F32)
    return result


def shards(tokens, teacher, expert_ids, route_gates, placement, gate_up_weight, down_weight):
    rows = tokens.shape[0]
    w_gu = gate_up_weight[0]
    w_dn = down_weight[0]
    ff = w_dn.shape[0]
    count = lax.axis_size("expert")
    here = lax.axis_index("expert")
    y_at, z_at, c_at = here // 4, (here // 2) % 2, here % 2

    table = jnp.arange(count, dtype=jnp.int32)
    chosen = expert_ids[:, :, None] == table
    position = jnp.sum(jnp.where(chosen, placement, 0), axis=2)
    gate_of = jnp.sum(
        jnp.where(table[:, None, None] == position[None], route_gates[None], 0.0), axis=2
    )

    far_rows = from_expert(tokens, 0, 1, 0)
    near = gather_y(tokens)
    gate_in = lax.all_to_all(gate_of, "expert", split_axis=0, concat_axis=0, tiled=True)
    near, far_rows, gate_in = tie(near, far_rows, gate_in)

    def gates(dz, dc):
        out = []
        for dy in range(NY):
            src = ((y_at + dy) % NY) * 4 + (z_at ^ dz) * 2 + (c_at ^ dc)
            out.append(jnp.sum(jnp.where(table[:, None] == src, gate_in, 0.0), axis=0))
        return jnp.concatenate(out)[:, None]

    def forward(row_block, gate):
        pre = mm(row_block, w_gu, ((1,), (0,)))
        g, u = pre[:, :ff], pre[:, ff:]
        s = jax.nn.sigmoid(g)
        hidden = (gate * (g * s) * u).astype(BF)
        return pre, hidden, mm(hidden, w_dn, ((1,), (0,)))

    def backward(res_block, saved):
        pre, gate = saved
        g, u = pre[:, :ff], pre[:, ff:]
        s = jax.nn.sigmoid(g)
        grad = gate * mm(res_block, w_dn, ((1,), (1,)))
        at_gate = (grad * u * (s * (1.0 + g * (1.0 - s)))).astype(BF)
        at_up = (grad * (g * s)).astype(BF)
        mixed = jnp.concatenate([at_gate, at_up], axis=1)
        return at_gate, at_up, mm(mixed, w_gu, ((1,), (1,)))

    gate = [[gates(dz, dc) for dc in (0, 1)] for dz in (0, 1)]
    saved = [[None, None], [None, None]]
    hidden = [[None, None], [None, None]]

    far = gather_y(far_rows)
    row_blocks = [[near, across(near)], None]
    both = [None, None]
    for dz in (0, 1):
        if dz == 1:
            far, near_own = tie(far, both[0][0])
            row_blocks[1] = [far, across(far)]
        outs = [None, None]
        for dc in (1, 0):
            pre, hidden[dz][dc], outs[dc] = forward(row_blocks[dz][dc], gate[dz][dc])
            saved[dz][dc] = (pre, gate[dz][dc])
        both[dz] = joined(outs[0], outs[1], rows)
    far_sum = scatter_y(both[1], both[1][0])
    near_sum = scatter_y(both[0], near_own)
    layer_sum = near_sum + from_expert(far_sum.astype(BF), 0, 1, 0).astype(F32)
    layer_out = layer_sum.astype(BF)
    residual = (layer_sum - teacher.astype(F32)).astype(BF)

    far_res = from_expert(residual, 0, 1, 0)
    near_res = gather_y(residual)
    near_res, far_res = tie(near_res, far_res)
    far_res = gather_y(far_res)
    res = [near_res, across(near_res)]
    near_back = [backward(res[dc], saved[0][dc]) for dc in (0, 1)]
    near_both = joined(near_back[0][2], near_back[1][2], rows)
    near_sum = scatter_y(near_both, near_both[0])

    def sides(dz, back):
        out = []
        for dc in (0, 1):
            out += [back[dc][0], back[dc][1], hidden[dz][dc]]
        return out

    (term,) = weight_grads(row_blocks[0], res, sides(0, near_back), None)

    res = [far_res, across(far_res)]
    back = [backward(res[dc], saved[1][dc]) for dc in (0, 1)]
    blocks = weight_grads(row_blocks[1], res, sides(1, back), term)
    got = x_stage(blocks)
    far_both = joined(back[0][2], back[1][2], rows)
    far_sum = scatter_y(far_both, far_both[0]).astype(BF)
    crossed = from_expert(far_sum, 0, 1, 0)

    total = blocks[0].astype(F32)
    for part in got:
        total = total + part.astype(F32)
    share = z_stage(total)
    token_sum = near_sum + crossed.astype(F32)
    split = 2 * ff
    return (layer_out, token_sum.astype(BF), share[:split].T[None], share[split:][None])


def solution(mesh):
    in_specs = (
        P(("dp", "expert"), None),
        P(("dp", "expert"), None),
        P(("dp", "expert"), None),
        P(("dp", "expert"), None),
        P(),
        P("expert", None, None),
        P("expert", None, None),
    )
    out_specs = (
        P(("dp", "expert"), None),
        P(("dp", "expert"), None),
        P("expert", "dp", None),
        P("expert", None, "dp"),
    )

    return jax.shard_map(shards, mesh=mesh, in_specs=in_specs, out_specs=out_specs, check_vma=False)
```

```python
import jax
import jax.numpy as jnp
from jax import lax
from jax.experimental import pallas as pl
from jax.experimental.pallas import tpu as pltpu
from jax.sharding import PartitionSpec as P


BF = jnp.bfloat16
F32 = jnp.float32
NY = 4
NX = 4
NZ = 4


def expert_perm(dy, dz, dc):
    out = []
    for y in range(NY):
        for z in range(2):
            for c in range(2):
                src = ((y + dy) % NY) * 4 + (z ^ dz) * 2 + (c ^ dc)
                out.append((src, y * 4 + z * 2 + c))
    return out


def dp_perm(dzl, dx):
    out = []
    for z in range(NZ):
        for x in range(NX):
            src = ((z + dzl) % NZ) * NX + (x + dx) % NX
            out.append((src, z * NX + x))
    return out


def from_expert(value, dy, dz, dc):
    return lax.ppermute(value, "expert", expert_perm(dy, dz, dc))


def from_dp(value, dzl, dx):
    return lax.ppermute(value, "dp", dp_perm(dzl, dx))


def mm(a, b, dims):
    return lax.dot_general(a, b, (dims, ((), ())), preferred_element_type=F32)


def tie(*values):
    return lax.optimization_barrier(values)


def gather_y(start):
    blocks = [start] + [from_expert(start, dy, 0, 0) for dy in (2, 1, 3)]
    return jnp.concatenate([blocks[0], blocks[2], blocks[1], blocks[3]], axis=0)


def scatter_y(blocks, own):
    total = own.astype(F32)
    for dy in (2, 1, 3):
        total = total + from_expert(blocks[dy], -dy, 0, 0).astype(F32)
    return total


def across(value):
    return from_expert(value, 0, 0, 1)


def joined(part, other, rows):
    (part,) = tie(part.astype(BF))
    got = across(other.astype(BF))
    out = []
    for dy in range(NY):
        at = slice(dy * rows, (dy + 1) * rows)
        out.append((part[at].astype(F32) + got[at].astype(F32)).astype(BF))
    return out


LANES = 128


def grad_kernel(x_ref, *refs):
    columns, refs = refs[:16], refs[16:]
    sides, outs, turned = refs[:12], refs[12:-1], refs[-1]
    ff = sides[0].shape[1]

    @pl.when((pl.program_id(0) == 0) & (pl.program_id(1) == 0))
    def _():
        for k in range(12):
            turned[k] = sides[k][...].astype(F32).T.astype(BF)

    wide = [
        jnp.concatenate([columns[2 * k][...], columns[2 * k + 1][...]], axis=1) for k in range(8)
    ]

    def product(side, array):
        total = mm(turned[side], wide[array], ((1,), (0,)))
        for p in range(1, 4):
            total = total + mm(turned[3 * p + side], wide[array + p], ((1,), (0,)))
        return total.astype(BF)

    parts = [product(0, 0), product(1, 0), product(2, 4)]
    for k in range(NX):

        @pl.when(pl.program_id(0) == k)
        def _(k=k):
            for side in range(3):
                for z in range(2):
                    value = parts[side][:, z * LANES : (z + 1) * LANES]
                    outs[k][z, side * ff : (side + 1) * ff, :] = value


def weight_grads(row_blocks, res, sides):
    count, features = row_blocks[0].shape
    ff = sides[0].shape[1]
    x_at = (lax.axis_index("dp") % NX).astype(jnp.int32).reshape(1)

    def column(second):
        return pl.BlockSpec(
            (count, LANES),
            lambda i, j, x: (0, (2 * j + second) * NX + (x[0] + i) % NX),
        )

    def block_of(k):
        def index(i, j, x):
            return (jnp.where(i == k, j, jnp.where(i < k, 0, 1)), 0, 0)

        return pl.BlockSpec((2, 3 * ff, LANES), index)

    args, specs = [], []
    for array in (*row_blocks, *res):
        args += [array, array]
        specs += [column(0), column(1)]
    args += sides
    specs += [pl.BlockSpec((count, ff), lambda i, j, x: (0, 0))] * 12
    return pl.pallas_call(
        grad_kernel,
        grid_spec=pltpu.PrefetchScalarGridSpec(
            num_scalar_prefetch=1,
            grid=(NX, NZ // 2),
            in_specs=specs,
            out_specs=[block_of(k) for k in range(NX)],
            scratch_shapes=[pltpu.VMEM((12, ff, count), BF)],
        ),
        out_shape=[jax.ShapeDtypeStruct((NZ, 3 * ff, LANES), BF)] * NX,
        name="weight_grads",
        cost_estimate=pl.CostEstimate(
            flops=24 * count * features * ff,
            transcendentals=0,
            bytes_accessed=16 * count * features + 12 * features * ff,
        ),
    )(x_at, *args)


def x_stage(blocks):
    half = NZ // 2
    low, high = slice(0, half), slice(half, None)
    via_low = from_dp(blocks[2][low], 0, -1)
    via_high = from_dp(blocks[2][high], 0, 1)
    up_high = from_dp(blocks[1][high], 0, -1)
    down_low = from_dp(blocks[3][low], 0, 1)
    up = (blocks[1][low].astype(F32) + via_low.astype(F32)).astype(BF)
    down = (blocks[3][high].astype(F32) + via_high.astype(F32)).astype(BF)
    up_low = from_dp(up, 0, -1)
    down_high = from_dp(down, 0, 1)
    return [jnp.concatenate([up_low, up_high]), jnp.concatenate([down_low, down_high])]


def z_stage(total):
    z_at = lax.axis_index("dp") // NX
    result = lax.dynamic_index_in_dim(total, z_at, 0, keepdims=False)
    rounded = total.astype(BF)
    for dzl in (2, 1, 3):
        part = lax.dynamic_index_in_dim(rounded, (z_at + dzl) % NZ, 0, keepdims=False)
        result = result + from_dp(part, -dzl, 0).astype(F32)
    return result


def shards(tokens, teacher, expert_ids, route_gates, placement, gate_up_weight, down_weight):
    rows = tokens.shape[0]
    w_gu = gate_up_weight[0]
    w_dn = down_weight[0]
    ff = w_dn.shape[0]
    count = lax.axis_size("expert")
    here = lax.axis_index("expert")
    y_at, z_at, c_at = here // 4, (here // 2) % 2, here % 2

    table = jnp.arange(count, dtype=jnp.int32)
    chosen = expert_ids[:, :, None] == table
    position = jnp.sum(jnp.where(chosen, placement, 0), axis=2)
    gate_of = jnp.sum(
        jnp.where(table[:, None, None] == position[None], route_gates[None], 0.0), axis=2
    )

    far_rows = from_expert(tokens, 0, 1, 0)
    near = gather_y(tokens)
    gate_in = lax.all_to_all(gate_of, "expert", split_axis=0, concat_axis=0, tiled=True)
    near, far_rows, gate_in = tie(near, far_rows, gate_in)

    def gates(dz, dc):
        out = []
        for dy in range(NY):
            src = ((y_at + dy) % NY) * 4 + (z_at ^ dz) * 2 + (c_at ^ dc)
            out.append(jnp.sum(jnp.where(table[:, None] == src, gate_in, 0.0), axis=0))
        return jnp.concatenate(out)[:, None]

    def forward(row_block, gate):
        pre = mm(row_block, w_gu, ((1,), (0,)))
        g, u = pre[:, :ff], pre[:, ff:]
        s = jax.nn.sigmoid(g)
        hidden = (gate * (g * s) * u).astype(BF)
        return pre, hidden, mm(hidden, w_dn, ((1,), (0,)))

    def backward(res_block, saved):
        pre, gate = saved
        g, u = pre[:, :ff], pre[:, ff:]
        s = jax.nn.sigmoid(g)
        grad = gate * mm(res_block, w_dn, ((1,), (1,)))
        at_gate = (grad * u * (s * (1.0 + g * (1.0 - s)))).astype(BF)
        at_up = (grad * (g * s)).astype(BF)
        mixed = jnp.concatenate([at_gate, at_up], axis=1)
        return at_gate, at_up, mm(mixed, w_gu, ((1,), (1,)))

    gate = [[gates(dz, dc) for dc in (0, 1)] for dz in (0, 1)]
    saved = [[None, None], [None, None]]
    hidden = [[None, None], [None, None]]

    far = gather_y(far_rows)
    row_blocks = [[near, across(near)], None]
    both = [None, None]
    for dz in (0, 1):
        if dz == 1:
            far, near_own = tie(far, both[0][0])
            row_blocks[1] = [far, across(far)]
        outs = [None, None]
        for dc in (1, 0):
            pre, hidden[dz][dc], outs[dc] = forward(row_blocks[dz][dc], gate[dz][dc])
            saved[dz][dc] = (pre, gate[dz][dc])
        both[dz] = joined(outs[0], outs[1], rows)
    far_sum = scatter_y(both[1], both[1][0])
    near_sum = scatter_y(both[0], near_own)
    layer_sum = near_sum + from_expert(far_sum.astype(BF), 0, 1, 0).astype(F32)
    layer_out = layer_sum.astype(BF)
    residual = (layer_sum - teacher.astype(F32)).astype(BF)

    far_res = from_expert(residual, 0, 1, 0)
    near_res = gather_y(residual)
    near_res, far_res = tie(near_res, far_res)
    far_res = gather_y(far_res)
    res = [near_res, across(near_res)]
    near_back = [backward(res[dc], saved[0][dc]) for dc in (0, 1)]
    near_both = joined(near_back[0][2], near_back[1][2], rows)
    near_sum = scatter_y(near_both, near_both[0])

    def sides(dz, back):
        out = []
        for dc in (0, 1):
            out += [back[dc][0], back[dc][1], hidden[dz][dc]]
        return out

    all_res = [*res, far_res, across(far_res)]
    back = [backward(all_res[2 + dc], saved[1][dc]) for dc in (0, 1)]
    blocks = weight_grads(
        [*row_blocks[0], *row_blocks[1]], all_res, sides(0, near_back) + sides(1, back)
    )
    got = x_stage(blocks)
    far_both = joined(back[0][2], back[1][2], rows)
    far_sum = scatter_y(far_both, far_both[0]).astype(BF)
    crossed = from_expert(far_sum, 0, 1, 0)

    total = blocks[0].astype(F32)
    for part in got:
        total = total + part.astype(F32)
    share = z_stage(total)
    token_sum = near_sum + crossed.astype(F32)
    split = 2 * ff
    return (layer_out, token_sum.astype(BF), share[:split].T[None], share[split:][None])


def solution(mesh):
    in_specs = (
        P(("dp", "expert"), None),
        P(("dp", "expert"), None),
        P(("dp", "expert"), None),
        P(("dp", "expert"), None),
        P(),
        P("expert", None, None),
        P("expert", None, None),
    )
    out_specs = (
        P(("dp", "expert"), None),
        P(("dp", "expert"), None),
        P("expert", "dp", None),
        P("expert", None, "dp"),
    )

    return jax.shard_map(shards, mesh=mesh, in_specs=in_specs, out_specs=out_specs, check_vma=False)
```

```python
import functools

import jax
import jax.numpy as jnp
from jax import lax
from jax.experimental import pallas as pl
from jax.experimental.pallas import tpu as pltpu
from jax.sharding import PartitionSpec as P


BF = jnp.bfloat16
F32 = jnp.float32
NY = 4
NX = 4
NZ = 4


def expert_perm(dy, dz, dc):
    out = []
    for y in range(NY):
        for z in range(2):
            for c in range(2):
                src = ((y + dy) % NY) * 4 + (z ^ dz) * 2 + (c ^ dc)
                out.append((src, y * 4 + z * 2 + c))
    return out


def dp_perm(dzl, dx):
    out = []
    for z in range(NZ):
        for x in range(NX):
            src = ((z + dzl) % NZ) * NX + (x + dx) % NX
            out.append((src, z * NX + x))
    return out


def from_expert(value, dy, dz, dc):
    return lax.ppermute(value, "expert", expert_perm(dy, dz, dc))


def from_dp(value, dzl, dx):
    return lax.ppermute(value, "dp", dp_perm(dzl, dx))


def mm(a, b, dims):
    return lax.dot_general(a, b, (dims, ((), ())), preferred_element_type=F32)


def tie(*values):
    return lax.optimization_barrier(values)


def gather_y(start):
    blocks = [start] + [from_expert(start, dy, 0, 0) for dy in (2, 1, 3)]
    return jnp.concatenate([blocks[0], blocks[2], blocks[1], blocks[3]], axis=0)


def scatter_y(blocks, own):
    total = own.astype(F32)
    for dy in (2, 1, 3):
        total = total + from_expert(blocks[dy], -dy, 0, 0).astype(F32)
    return total


def across(value):
    return from_expert(value, 0, 0, 1)


def joined(part, other, rows):
    (part,) = tie(part.astype(BF))
    got = across(other.astype(BF))
    out = []
    for dy in range(NY):
        at = slice(dy * rows, (dy + 1) * rows)
        out.append((part[at].astype(F32) + got[at].astype(F32)).astype(BF))
    return out


LANES = 128


def grad_kernel(x_ref, *refs, first):
    rows, res, sides = refs[:2], refs[2:4], refs[4:10]
    acc, refs = (None, refs[10:]) if first else (refs[10], refs[11:])
    out, turned = refs
    ff = sides[0].shape[1]

    @pl.when(pl.program_id(0) == 0)
    def _():
        for k in range(6):
            turned[k] = sides[k][...].astype(F32).T.astype(BF)

    for side in range(3):
        right = res if side == 2 else rows
        at = slice(side * ff, (side + 1) * ff)
        total = mm(turned[side], right[0][...], ((1,), (0,)))
        total = total + mm(turned[3 + side], right[1][...], ((1,), (0,)))
        if first:
            out[at, :] = total
        else:
            total = (total + acc[at, :]).astype(BF)
            for x in range(NX):
                out[lax.rem(x - x_ref[0] + NX, NX), 0, at, :] = total[:, x * LANES : (x + 1) * LANES]


def weight_grads(row_blocks, res, sides, acc):
    count, features = row_blocks[0].shape
    ff = sides[0].shape[1]
    tile = NX * LANES
    x_at = (lax.axis_index("dp") % NX).astype(jnp.int32).reshape(1)
    args = [*row_blocks, *res, *sides]
    specs = [pl.BlockSpec((count, tile), lambda j, x: (0, j))] * 4
    specs += [pl.BlockSpec((count, ff), lambda j, x: (0, 0))] * 6
    acc_spec = pl.BlockSpec((3 * ff, tile), lambda j, x: (0, j))
    if acc is None:
        out_spec = acc_spec
        out_shape = jax.ShapeDtypeStruct((3 * ff, features), F32)
    else:
        args.append(acc)
        specs.append(acc_spec)
        out_spec = pl.BlockSpec((NX, 1, 3 * ff, LANES), lambda j, x: (0, j, 0, 0))
        out_shape = jax.ShapeDtypeStruct((NX, NZ, 3 * ff, LANES), BF)
    return pl.pallas_call(
        functools.partial(grad_kernel, first=acc is None),
        grid_spec=pltpu.PrefetchScalarGridSpec(
            num_scalar_prefetch=1,
            grid=(NZ,),
            in_specs=specs,
            out_specs=out_spec,
            scratch_shapes=[pltpu.VMEM((6, ff, count), BF)],
        ),
        out_shape=out_shape,
        name="weight_grads",
        cost_estimate=pl.CostEstimate(
            flops=12 * count * features * ff,
            transcendentals=0,
            bytes_accessed=8 * count * features + 18 * features * ff,
        ),
    )(x_at, *args)


def x_stage(blocks):
    half = NZ // 2
    low, high = slice(0, half), slice(half, None)
    via_low = from_dp(blocks[2][low], 0, -1)
    via_high = from_dp(blocks[2][high], 0, 1)
    up_high = from_dp(blocks[1][high], 0, -1)
    down_low = from_dp(blocks[3][low], 0, 1)
    up = (blocks[1][low].astype(F32) + via_low.astype(F32)).astype(BF)
    down = (blocks[3][high].astype(F32) + via_high.astype(F32)).astype(BF)
    up_low = from_dp(up, 0, -1)
    down_high = from_dp(down, 0, 1)
    return [jnp.concatenate([up_low, up_high]), jnp.concatenate([down_low, down_high])]


def z_stage(total):
    z_at = lax.axis_index("dp") // NX
    result = lax.dynamic_index_in_dim(total, z_at, 0, keepdims=False)
    rounded = total.astype(BF)
    for dzl in (2, 1, 3):
        part = lax.dynamic_index_in_dim(rounded, (z_at + dzl) % NZ, 0, keepdims=False)
        result = result + from_dp(part, -dzl, 0).astype(F32)
    return result


def shards(tokens, teacher, expert_ids, route_gates, placement, gate_up_weight, down_weight):
    rows = tokens.shape[0]
    w_gu = gate_up_weight[0]
    w_dn = down_weight[0]
    ff = w_dn.shape[0]
    count = lax.axis_size("expert")
    here = lax.axis_index("expert")
    y_at, z_at, c_at = here // 4, (here // 2) % 2, here % 2

    table = jnp.arange(count, dtype=jnp.int32)
    chosen = expert_ids[:, :, None] == table
    position = jnp.sum(jnp.where(chosen, placement, 0), axis=2)
    gate_of = jnp.sum(
        jnp.where(table[:, None, None] == position[None], route_gates[None], 0.0), axis=2
    )

    far_rows = from_expert(tokens, 0, 1, 0)
    near = gather_y(tokens)
    gate_in = lax.all_to_all(gate_of, "expert", split_axis=0, concat_axis=0, tiled=True)
    near, far_rows, gate_in = tie(near, far_rows, gate_in)

    def gates(dz, dc):
        out = []
        for dy in range(NY):
            src = ((y_at + dy) % NY) * 4 + (z_at ^ dz) * 2 + (c_at ^ dc)
            out.append(jnp.sum(jnp.where(table[:, None] == src, gate_in, 0.0), axis=0))
        return jnp.concatenate(out)[:, None]

    def forward(row_block, gate):
        pre = mm(row_block, w_gu, ((1,), (0,)))
        g, u = pre[:, :ff], pre[:, ff:]
        s = jax.nn.sigmoid(g)
        hidden = (gate * (g * s) * u).astype(BF)
        return pre, hidden, mm(hidden, w_dn, ((1,), (0,)))

    def backward(res_block, saved):
        pre, gate = saved
        g, u = pre[:, :ff], pre[:, ff:]
        s = jax.nn.sigmoid(g)
        grad = gate * mm(res_block, w_dn, ((1,), (1,)))
        at_gate = (grad * u * (s * (1.0 + g * (1.0 - s)))).astype(BF)
        at_up = (grad * (g * s)).astype(BF)
        mixed = jnp.concatenate([at_gate, at_up], axis=1)
        return at_gate, at_up, mm(mixed, w_gu, ((1,), (1,)))

    gate = [[gates(dz, dc) for dc in (0, 1)] for dz in (0, 1)]
    saved = [[None, None], [None, None]]
    hidden = [[None, None], [None, None]]

    far = gather_y(far_rows)
    row_blocks = [[near, across(near)], None]
    both = [None, None]
    for dz in (0, 1):
        if dz == 1:
            far, near_own = tie(far, both[0][0])
            row_blocks[1] = [far, across(far)]
        outs = [None, None]
        for dc in (1, 0):
            pre, hidden[dz][dc], outs[dc] = forward(row_blocks[dz][dc], gate[dz][dc])
            saved[dz][dc] = (pre, gate[dz][dc])
        both[dz] = joined(outs[0], outs[1], rows)
    far_sum = scatter_y(both[1], both[1][0])
    near_sum = scatter_y(both[0], near_own)
    layer_sum = near_sum + from_expert(far_sum.astype(BF), 0, 1, 0).astype(F32)
    layer_out = layer_sum.astype(BF)
    residual = (layer_sum - teacher.astype(F32)).astype(BF)

    far_res = from_expert(residual, 0, 1, 0)
    near_res = gather_y(residual)
    near_res, far_res = tie(near_res, far_res)
    far_res = gather_y(far_res)
    res = [near_res, across(near_res)]
    near_back = [backward(res[dc], saved[0][dc]) for dc in (0, 1)]
    near_both = joined(near_back[0][2], near_back[1][2], rows)
    near_sum = scatter_y(near_both, near_both[0])

    def sides(dz, back):
        out = []
        for dc in (0, 1):
            out += [back[dc][0], back[dc][1], hidden[dz][dc]]
        return out

    term = weight_grads(row_blocks[0], res, sides(0, near_back), None)

    res = [far_res, across(far_res)]
    back = [backward(res[dc], saved[1][dc]) for dc in (0, 1)]
    blocks = weight_grads(row_blocks[1], res, sides(1, back), term)
    got = x_stage(blocks)
    far_both = joined(back[0][2], back[1][2], rows)
    far_sum = scatter_y(far_both, far_both[0]).astype(BF)
    crossed = from_expert(far_sum, 0, 1, 0)

    total = blocks[0].astype(F32)
    for part in got:
        total = total + part.astype(F32)
    share = z_stage(total)
    token_sum = near_sum + crossed.astype(F32)
    split = 2 * ff
    return (layer_out, token_sum.astype(BF), share[:split].T[None], share[split:][None])


def solution(mesh):
    in_specs = (
        P(("dp", "expert"), None),
        P(("dp", "expert"), None),
        P(("dp", "expert"), None),
        P(("dp", "expert"), None),
        P(),
        P("expert", None, None),
        P("expert", None, None),
    )
    out_specs = (
        P(("dp", "expert"), None),
        P(("dp", "expert"), None),
        P("expert", "dp", None),
        P("expert", None, "dp"),
    )

    return jax.shard_map(shards, mesh=mesh, in_specs=in_specs, out_specs=out_specs, check_vma=False)
```

```python
import jax
import jax.numpy as jnp
from jax import lax
from jax.experimental import pallas as pl
from jax.experimental.pallas import tpu as pltpu
from jax.sharding import PartitionSpec as P


BF = jnp.bfloat16
F32 = jnp.float32
NY = 4
NX = 4
NZ = 4


def expert_perm(dy, dz, dc):
    out = []
    for y in range(NY):
        for z in range(2):
            for c in range(2):
                src = ((y + dy) % NY) * 4 + (z ^ dz) * 2 + (c ^ dc)
                out.append((src, y * 4 + z * 2 + c))
    return out


def dp_perm(dzl, dx):
    out = []
    for z in range(NZ):
        for x in range(NX):
            src = ((z + dzl) % NZ) * NX + (x + dx) % NX
            out.append((src, z * NX + x))
    return out


def from_expert(value, dy, dz, dc):
    return lax.ppermute(value, "expert", expert_perm(dy, dz, dc))


def from_dp(value, dzl, dx):
    return lax.ppermute(value, "dp", dp_perm(dzl, dx))


def mm(a, b, dims):
    return lax.dot_general(a, b, (dims, ((), ())), preferred_element_type=F32)


def tie(*values):
    return lax.optimization_barrier(values)


def gather_y(start):
    blocks = [start] + [from_expert(start, dy, 0, 0) for dy in (2, 1, 3)]
    return jnp.concatenate([blocks[0], blocks[2], blocks[1], blocks[3]], axis=0)


def scatter_y(blocks, own):
    total = own.astype(F32)
    for dy in (2, 1, 3):
        total = total + from_expert(blocks[dy], -dy, 0, 0).astype(F32)
    return total


def across(value):
    return from_expert(value, 0, 0, 1)


def joined(part, other, rows):
    (part,) = tie(part.astype(BF))
    got = across(other.astype(BF))
    out = []
    for dy in range(NY):
        at = slice(dy * rows, (dy + 1) * rows)
        out.append((part[at].astype(F32) + got[at].astype(F32)).astype(BF))
    return out


LANES = 128


def grad_kernel(x_ref, *refs):
    rows, res, sides, out, turned = refs[:4], refs[4:8], refs[8:20], refs[20], refs[21]
    ff = sides[0].shape[1]

    @pl.when(pl.program_id(0) == 0)
    def _():
        for k in range(12):
            turned[k] = sides[k][...].astype(F32).T.astype(BF)

    for side in range(3):
        right = res if side == 2 else rows
        at = slice(side * ff, (side + 1) * ff)
        total = mm(turned[side], right[0][...], ((1,), (0,)))
        for p in range(1, 4):
            total = total + mm(turned[3 * p + side], right[p][...], ((1,), (0,)))
        total = total.astype(BF)
        for x in range(NX):
            out[lax.rem(x - x_ref[0] + NX, NX), 0, at, :] = total[:, x * LANES : (x + 1) * LANES]


def weight_grads(row_blocks, res, sides):
    count, features = row_blocks[0].shape
    ff = sides[0].shape[1]
    x_at = (lax.axis_index("dp") % NX).astype(jnp.int32).reshape(1)
    specs = [pl.BlockSpec((count, NX * LANES), lambda j, x: (0, j))] * 8
    once = pl.BlockSpec((count, ff), lambda j, x: (0, 0), pipeline_mode=pl.Buffered(1))
    return pl.pallas_call(
        grad_kernel,
        grid_spec=pltpu.PrefetchScalarGridSpec(
            num_scalar_prefetch=1,
            grid=(NZ,),
            in_specs=specs + [once] * 12,
            out_specs=pl.BlockSpec((NX, 1, 3 * ff, LANES), lambda j, x: (0, j, 0, 0)),
            scratch_shapes=[pltpu.VMEM((12, ff, count), BF)],
        ),
        out_shape=jax.ShapeDtypeStruct((NX, NZ, 3 * ff, LANES), BF),
        name="weight_grads",
        cost_estimate=pl.CostEstimate(
            flops=24 * count * features * ff,
            transcendentals=0,
            bytes_accessed=16 * count * features + 12 * features * ff,
        ),
    )(x_at, *row_blocks, *res, *sides)


def x_stage(blocks):
    half = NZ // 2
    low, high = slice(0, half), slice(half, None)
    via_low = from_dp(blocks[2][low], 0, -1)
    via_high = from_dp(blocks[2][high], 0, 1)
    up_high = from_dp(blocks[1][high], 0, -1)
    down_low = from_dp(blocks[3][low], 0, 1)
    up = (blocks[1][low].astype(F32) + via_low.astype(F32)).astype(BF)
    down = (blocks[3][high].astype(F32) + via_high.astype(F32)).astype(BF)
    up_low = from_dp(up, 0, -1)
    down_high = from_dp(down, 0, 1)
    return [jnp.concatenate([up_low, up_high]), jnp.concatenate([down_low, down_high])]


def z_stage(total):
    z_at = lax.axis_index("dp") // NX
    result = lax.dynamic_index_in_dim(total, z_at, 0, keepdims=False)
    rounded = total.astype(BF)
    for dzl in (2, 1, 3):
        part = lax.dynamic_index_in_dim(rounded, (z_at + dzl) % NZ, 0, keepdims=False)
        result = result + from_dp(part, -dzl, 0).astype(F32)
    return result


def shards(tokens, teacher, expert_ids, route_gates, placement, gate_up_weight, down_weight):
    rows = tokens.shape[0]
    w_gu = gate_up_weight[0]
    w_dn = down_weight[0]
    ff = w_dn.shape[0]
    count = lax.axis_size("expert")
    here = lax.axis_index("expert")
    y_at, z_at, c_at = here // 4, (here // 2) % 2, here % 2

    table = jnp.arange(count, dtype=jnp.int32)
    chosen = expert_ids[:, :, None] == table
    position = jnp.sum(jnp.where(chosen, placement, 0), axis=2)
    gate_of = jnp.sum(
        jnp.where(table[:, None, None] == position[None], route_gates[None], 0.0), axis=2
    )

    far_rows = from_expert(tokens, 0, 1, 0)
    near = gather_y(tokens)
    gate_in = lax.all_to_all(gate_of, "expert", split_axis=0, concat_axis=0, tiled=True)
    near, far_rows, gate_in = tie(near, far_rows, gate_in)

    def gates(dz, dc):
        out = []
        for dy in range(NY):
            src = ((y_at + dy) % NY) * 4 + (z_at ^ dz) * 2 + (c_at ^ dc)
            out.append(jnp.sum(jnp.where(table[:, None] == src, gate_in, 0.0), axis=0))
        return jnp.concatenate(out)[:, None]

    def forward(row_block, gate):
        pre = mm(row_block, w_gu, ((1,), (0,)))
        g, u = pre[:, :ff], pre[:, ff:]
        s = jax.nn.sigmoid(g)
        hidden = (gate * (g * s) * u).astype(BF)
        return pre, hidden, mm(hidden, w_dn, ((1,), (0,)))

    def backward(res_block, saved):
        pre, gate = saved
        g, u = pre[:, :ff], pre[:, ff:]
        s = jax.nn.sigmoid(g)
        grad = gate * mm(res_block, w_dn, ((1,), (1,)))
        at_gate = (grad * u * (s * (1.0 + g * (1.0 - s)))).astype(BF)
        at_up = (grad * (g * s)).astype(BF)
        mixed = jnp.concatenate([at_gate, at_up], axis=1)
        return at_gate, at_up, mm(mixed, w_gu, ((1,), (1,)))

    gate = [[gates(dz, dc) for dc in (0, 1)] for dz in (0, 1)]
    saved = [[None, None], [None, None]]
    hidden = [[None, None], [None, None]]

    far = gather_y(far_rows)
    row_blocks = [[near, across(near)], None]
    both = [None, None]
    for dz in (0, 1):
        if dz == 1:
            far, near_own = tie(far, both[0][0])
            row_blocks[1] = [far, across(far)]
        outs = [None, None]
        for dc in (1, 0):
            pre, hidden[dz][dc], outs[dc] = forward(row_blocks[dz][dc], gate[dz][dc])
            saved[dz][dc] = (pre, gate[dz][dc])
        both[dz] = joined(outs[0], outs[1], rows)
    far_sum = scatter_y(both[1], both[1][0])
    near_sum = scatter_y(both[0], near_own)
    layer_sum = near_sum + from_expert(far_sum.astype(BF), 0, 1, 0).astype(F32)
    layer_out = layer_sum.astype(BF)
    residual = (layer_sum - teacher.astype(F32)).astype(BF)

    far_res = from_expert(residual, 0, 1, 0)
    near_res = gather_y(residual)
    near_res, far_res = tie(near_res, far_res)
    far_res = gather_y(far_res)
    res = [near_res, across(near_res)]
    near_back = [backward(res[dc], saved[0][dc]) for dc in (0, 1)]
    near_both = joined(near_back[0][2], near_back[1][2], rows)
    near_sum = scatter_y(near_both, near_both[0])

    def sides(dz, back):
        out = []
        for dc in (0, 1):
            out += [back[dc][0], back[dc][1], hidden[dz][dc]]
        return out

    all_res = [*res, far_res, across(far_res)]
    back = [backward(all_res[2 + dc], saved[1][dc]) for dc in (0, 1)]
    blocks = weight_grads(
        [*row_blocks[0], *row_blocks[1]], all_res, sides(0, near_back) + sides(1, back)
    )
    got = x_stage(blocks)
    far_both = joined(back[0][2], back[1][2], rows)
    far_sum = scatter_y(far_both, far_both[0]).astype(BF)
    crossed = from_expert(far_sum, 0, 1, 0)

    total = blocks[0].astype(F32)
    for part in got:
        total = total + part.astype(F32)
    share = z_stage(total)
    token_sum = near_sum + crossed.astype(F32)
    split = 2 * ff
    return (layer_out, token_sum.astype(BF), share[:split].T[None], share[split:][None])


def solution(mesh):
    in_specs = (
        P(("dp", "expert"), None),
        P(("dp", "expert"), None),
        P(("dp", "expert"), None),
        P(("dp", "expert"), None),
        P(),
        P("expert", None, None),
        P("expert", None, None),
    )
    out_specs = (
        P(("dp", "expert"), None),
        P(("dp", "expert"), None),
        P("expert", "dp", None),
        P("expert", None, "dp"),
    )

    return jax.shard_map(shards, mesh=mesh, in_specs=in_specs, out_specs=out_specs, check_vma=False)
```
